32 devices in a mesh: blk: 4 (over y, x), strata: 8 (over z, core).
Axes of the slice: x: 2, y: 2, z: 4, core: 2. Of those that a mesh axis runs over, the one named last changes fastest.
Arguments:
- user_factors: bfloat16 [4096, 256], P('blk'), may hold values from -1.5 to 1.5
- item_factors: bfloat16 [8192, 256], P(('blk', 'strata')), may hold values from -1.5 to 1.5
- ratings: bfloat16 [4, 4, 8, 8, 128, 128], P('blk', None, 'strata'), may hold values from -6 to 6
- tile_user: int32 [4, 4, 8, 8], P('blk', None, 'strata'), may hold values from 0 to 7
- tile_item: int32 [4, 4, 8, 8], P('blk', None, 'strata'), may hold values from 0 to 1
- tile_count: int32 [4, 4, 8], P('blk', None, 'strata'), may hold values from 1 to 8, 40 in all within a row
Outputs:
- user_grad: float32 [4096, 256], P('blk')
- item_grad: float32 [8192, 256], P(('blk', 'strata'))
The draws below stay inside these ranges and needn't reach their ends.
Inputs may be any that keep to these rules, and one draw needn't show every extreme that they name: `tile_count`: for each user block and panel index, the counts over the strata are uneven and one of them equals 8.
All inputs are finite; a program needn't handle non-finite values.
Results may differ from the reference program's by a relative error of at most 0.0012.
Values may be sent and summed in bfloat16 or wider, within the bound.
A program may use at most 64 MiB of HBM per device.

```python
import math
import jax
import jax.numpy as jnp
import numpy as np
from jax import lax

R = 256
TILE = 128
TILES = 8
UT = 8
PT = 2
USERS = 4096
ITEMS = 8192
N_BLK = 4
N_STRATA = 8


def touch_ends(values, stream_key, low, top_value):
    shape = values.shape
    place = [jax.random.randint(jax.random.fold_in(stream_key, axis), (), 0, shape[axis]) for axis in range(len(shape))]
    values = values.at[tuple(place)].set(low)
    longest = shape.index(max(shape))
    place[longest] = (place[longest] + 1) % shape[longest]
    return values.at[tuple(place)].set(top_value)


def level_of(stream_key, dims, pieces, low, largest):
    loudness = 1.0
    for position, blocks in pieces:
        draws = jax.random.uniform(jax.random.fold_in(jax.random.fold_in(stream_key, 6), position), (blocks,), jnp.float32, low / len(pieces), largest / len(pieces))
        loudness = loudness * jnp.repeat(jnp.exp(draws), dims[position] // blocks).reshape((-1,) + (1,) * (len(dims) - 1 - position))
    return loudness


def profile(count, total, most, skew):
    loads = [(1 << 20) // math.isqrt(grade ** skew) + 1 for grade in range(2, count + 1)]
    surplus, counts = total - most - (count - 1), [1] * (count - 1)
    while surplus > 0:
        free = [i for i in range(count - 1) if counts[i] < most]
        whole, left = sum([loads[i] for i in free]), surplus
        for i in free:
            extra = min(most - counts[i], max(1, left * loads[i] // whole), surplus)
            counts[i] = counts[i] + extra
            surplus = surplus - extra
    return np.array([most] + counts)


def uneven_parts(key, number_of, total, bound, slope):
    if number_of == 2:
        one = jax.random.randint(key, (), max(1, total - bound), min(bound, total - 1) + 1)
        return jnp.stack([one, total - one])
    sizes = jnp.asarray(profile(number_of, total, bound, slope), jnp.int32)
    twos = (number_of - 1) // 2
    giver, receiver = sizes[1:1 + 2 * twos:2], sizes[2:2 + 2 * twos:2]
    margin = jnp.minimum(giver - 1, bound - receiver)
    moved = jax.random.randint(jax.random.fold_in(key, 1), (twos,), 0, 1 << 20) % (margin + 1)
    sizes = sizes.at[1:1 + 2 * twos:2].set(giver - moved).at[2:2 + 2 * twos:2].set(receiver + moved)
    return sizes[jax.random.permutation(jax.random.fold_in(key, 2), number_of)]


def noise(own_key, dims, deviation, limit, split=(), held_as=jnp.bfloat16):
    loudness = level_of(own_key, dims, split, -0.22, 0.18) if split else 1.0
    drawn = jax.random.normal(own_key, dims, jnp.float32) * deviation * loudness
    return jnp.minimum(jnp.maximum(drawn, -limit), limit).astype(held_as)


def setup_inputs(seed: int = 0) -> dict:
    streams_of = jax.random.split(jax.random.key(seed), 7)
    user_factors = noise(streams_of[0], (USERS, R), 0.25, 1.5, ((0, 4),))
    item_factors = noise(streams_of[1], (ITEMS, R), 0.25, 1.5, ((0, 32),))
    ratings = noise(streams_of[2], (N_BLK, N_BLK, N_STRATA, TILES, TILE, TILE), 1.0, 6.0, ((0, 4), (2, 8)))
    tile_user = touch_ends(jax.random.randint(streams_of[3], (N_BLK, N_BLK, N_STRATA, TILES), 0, UT), jax.random.fold_in(streams_of[3], 1), 0, UT - 1).astype(jnp.int32)
    tile_item = touch_ends(jax.random.randint(streams_of[4], (N_BLK, N_BLK, N_STRATA, TILES), 0, PT), jax.random.fold_in(streams_of[4], 1), 0, PT - 1).astype(jnp.int32)
    tile_count = jax.vmap(lambda own: uneven_parts(own, N_STRATA, N_STRATA * TILES * 5 // 8, TILES, 2))(jax.random.split(streams_of[5], N_BLK * N_BLK)).reshape((N_BLK, N_BLK, N_STRATA)).astype(jnp.int32)
    return {"user_factors": user_factors, "item_factors": item_factors, "ratings": ratings, "tile_user": tile_user, "tile_item": tile_item, "tile_count": tile_count}


def tile_terms(user_tiles, panel_tiles, rating_tiles, rows, cols, count):
    picked_users = jnp.take(user_tiles, rows, axis=0).astype(jnp.float32)
    picked_items = jnp.take(panel_tiles, cols, axis=0).astype(jnp.float32)
    predicted = jnp.einsum('kar,kbr->kab', picked_users, picked_items, precision=lax.Precision.HIGHEST)
    live = (jnp.arange(TILES) < count).astype(jnp.float32)
    residue = ((predicted - rating_tiles.astype(jnp.float32)) * live[:, None, None]).astype(jnp.bfloat16)
    wide = residue.astype(jnp.float32)
    user_part = jnp.einsum('kab,kbr->kar', wide, picked_items, precision=lax.Precision.HIGHEST) / TILE
    item_part = jnp.einsum('kab,kar->kbr', wide, picked_users, precision=lax.Precision.HIGHEST) / TILE
    user_hot = (rows[:, None] == jnp.arange(UT)[None, :]).astype(jnp.float32)
    item_hot = (cols[:, None] == jnp.arange(PT)[None, :]).astype(jnp.float32)
    user_sum = jnp.einsum('ku,kar->uar', user_hot, user_part, precision=lax.Precision.HIGHEST)
    item_sum = jnp.einsum('kp,kbr->pbr', item_hot, item_part, precision=lax.Precision.HIGHEST)
    return user_sum, item_sum


def reference(user_factors, item_factors, ratings, tile_user, tile_item, tile_count):
    users = user_factors.reshape(N_BLK, UT, TILE, R)
    items = item_factors.reshape(N_BLK, N_STRATA, PT, TILE, R)
    strata_terms = jax.vmap(tile_terms, in_axes=(None, 0, 0, 0, 0, 0))

    def visit(pair, carry):
        user_total, item_total = carry
        owner = pair // N_BLK
        source = pair % N_BLK
        user_parts, item_parts = strata_terms(users[owner], items[source], ratings[owner, source],
                                              tile_user[owner, source], tile_item[owner, source],
                                              tile_count[owner, source])
        user_total = user_total.at[owner].add(jnp.sum(user_parts, axis=0))
        item_total = item_total.at[source].add(item_parts)
        return user_total, item_total

    start = (jnp.zeros((N_BLK, UT, TILE, R), jnp.float32), jnp.zeros((N_BLK, N_STRATA, PT, TILE, R), jnp.float32))
    user_total, item_total = lax.fori_loop(0, N_BLK * N_BLK, visit, start)
    return user_total.reshape(USERS, R), item_total.reshape(ITEMS, R)
```

```python
import functools

import jax
import jax.numpy as jnp
from jax import lax
from jax.experimental import pallas as pl
from jax.experimental.pallas import tpu as pltpu
from jax.sharding import PartitionSpec as P

MESH = pl.DeviceIdType.MESH
F32 = jnp.float32
BF16 = jnp.bfloat16
CHUNK = 64
LAG = 2


def flip(place, step, size):
    other, bit = 0, 1
    while bit < size:
        other = other + bit * ((place // bit + step // bit) % 2)
        bit *= 2
    return other


def kernel(
    n_blk,
    n_strata,
    users_hbm,
    items_hbm,
    ratings_hbm,
    rows_ref,
    cols_ref,
    count_ref,
    user_out,
    item_out,
    users,
    user_table,
    panels,
    panel,
    ratings,
    predicted,
    picked_items,
    picked_users,
    by_user,
    by_item,
    user_sum,
    item_send,
    item_recv,
    pair_recv,
    side_recv,
    side_send,
    load_sem,
    rating_sem,
    gather_send,
    gather_recv,
    item_send_sem,
    item_recv_sem,
    pair_send_sem,
    pair_recv_sem,
    side_send_sem,
    side_recv_sem,
    share_send_sem,
    share_recv_sem,
):
    tile = ratings.shape[-1]
    slots = ratings.shape[1]
    user_tiles = user_table.shape[0]
    panel_tiles = panel.shape[0]
    chunks = pair_recv.shape[0] // CHUNK
    per_tile = tile // CHUNK
    blk = lax.axis_index("blk")
    strata = lax.axis_index("strata")
    core = strata % 2
    sibling = strata + 1 - 2 * core
    chip = strata // 2
    chips = n_strata // 2
    half = chips // 2
    upper = chip // half
    sign = 1 - 2 * upper
    far = (chip + sign) * 2 + core
    near = (chip - sign) * 2 + core
    depth = chip + upper * (chips - 1 - 2 * chip)
    has_near = depth > 0
    crossing = depth // (half - 1) if half > 1 else depth + 1

    load = pltpu.make_async_copy(users_hbm, users, load_sem.at[0])
    load.start()
    load_panel = pltpu.make_async_copy(items_hbm, panels.at[0], load_sem.at[1])
    load_panel.start()

    def rating_copy(step):
        source = flip(blk, step, n_blk)
        return pltpu.make_async_copy(
            ratings_hbm.at[0, source, 0], ratings.at[step], rating_sem.at[step]
        )

    def start_rating(step, carry):
        rating_copy(step).start()
        return carry

    lax.fori_loop(0, n_blk, start_rating, 0)

    barrier = pltpu.get_barrier_semaphore()

    def greet(step, carry):
        pl.semaphore_signal(
            barrier, 1, device_id=(flip(blk, step, n_blk), strata), device_id_type=MESH
        )
        return carry

    lax.fori_loop(1, n_blk, greet, 0)
    pl.semaphore_signal(barrier, 1, device_id=(blk, sibling), device_id_type=MESH)
    pl.semaphore_signal(barrier, 1, device_id=(blk, far), device_id_type=MESH)

    @pl.when(has_near)
    def _():
        pl.semaphore_signal(barrier, 1, device_id=(blk, near), device_id_type=MESH)
        pl.semaphore_wait(barrier, n_blk + 2)

    @pl.when(depth == 0)
    def _():
        pl.semaphore_wait(barrier, n_blk + 1)

    def gather_copy(step):
        return pltpu.make_async_remote_copy(
            src_ref=items_hbm,
            dst_ref=panels.at[step],
            send_sem=gather_send.at[step],
            recv_sem=gather_recv.at[step],
            device_id=(flip(blk, step, n_blk), strata),
            device_id_type=MESH,
        )

    def item_copy(step):
        return pltpu.make_async_remote_copy(
            src_ref=item_send.at[step],
            dst_ref=item_recv.at[step],
            send_sem=item_send_sem.at[step],
            recv_sem=item_recv_sem.at[step],
            device_id=(flip(blk, step, n_blk), strata),
            device_id_type=MESH,
        )

    def pair_copy(q):
        return pltpu.make_async_remote_copy(
            src_ref=user_sum.at[pl.ds((2 * q + 1 - core) * tile, tile)],
            dst_ref=pair_recv.at[pl.ds(q * tile, tile)],
            send_sem=pair_send_sem.at[q],
            recv_sem=pair_recv_sem.at[q],
            device_id=(blk, sibling),
            device_id_type=MESH,
        )

    def far_copy(c):
        return pltpu.make_async_remote_copy(
            src_ref=side_send.at[0, c],
            dst_ref=side_recv.at[crossing, c],
            send_sem=side_send_sem.at[0, c],
            recv_sem=side_recv_sem.at[crossing, c],
            device_id=(blk, far),
            device_id_type=MESH,
        )

    def near_copy(c):
        return pltpu.make_async_remote_copy(
            src_ref=side_send.at[1, c],
            dst_ref=side_recv.at[1, c],
            send_sem=side_send_sem.at[1, c],
            recv_sem=side_recv_sem.at[1, c],
            device_id=(blk, near),
            device_id_type=MESH,
        )

    def arrived(side, c):
        return pltpu.make_async_remote_copy(
            src_ref=side_send.at[0, c],
            dst_ref=side_recv.at[side, c],
            send_sem=side_send_sem.at[0, c],
            recv_sem=side_recv_sem.at[side, c],
            device_id=(blk, far),
            device_id_type=MESH,
        )

    def own_rows(c, owner):
        return pl.ds((2 * (c // per_tile) + owner) * tile + (c % per_tile) * CHUNK, CHUNK)

    def share_copy(c):
        return pltpu.make_async_remote_copy(
            src_ref=user_out.at[own_rows(c, core)],
            dst_ref=user_out.at[own_rows(c, core)],
            send_sem=share_send_sem.at[c],
            recv_sem=share_recv_sem.at[c],
            device_id=(blk, sibling),
            device_id_type=MESH,
        )

    def share_arrival(c):
        return pltpu.make_async_remote_copy(
            src_ref=user_out.at[own_rows(c, core)],
            dst_ref=user_out.at[own_rows(c, 1 - core)],
            send_sem=share_send_sem.at[c],
            recv_sem=share_recv_sem.at[c],
            device_id=(blk, sibling),
            device_id_type=MESH,
        )

    def start_gather(step, carry):
        gather_copy(step).start()
        return carry

    lax.fori_loop(1, n_blk, start_gather, 0)
    user_sum[...] = jnp.zeros_like(user_sum)

    @pl.when(depth == 0)
    def _():
        side_recv[0] = jnp.zeros(side_recv.shape[1:], F32)

    load.wait()
    load_panel.wait()

    user_table[...] = users[...].reshape(user_table.shape)

    def hot(index, place):
        same = (index == place).astype(F32)
        return jnp.full((tile, tile), same, F32).astype(BF16)

    def visit(step, carry):
        source = flip(blk, step, n_blk)

        @pl.when(step > 0)
        def _():
            gather_copy(step).wait_recv()

        rating_copy(step).wait()
        panel[...] = panels[step].reshape(panel.shape)
        for u in range(user_tiles):
            product = lax.dot_general(
                users[u * tile : (u + 1) * tile],
                panels[step],
                (((1,), (1,)), ((), ())),
                preferred_element_type=F32,
            )
            for p in range(panel_tiles):
                predicted[u * panel_tiles + p] = product[:, p * tile : (p + 1) * tile]
        for k in range(slots):
            row = rows_ref[0, source, 0, k]
            col = cols_ref[0, source, 0, k]
            live = (k < count_ref[0, source, 0]).astype(F32)
            place = slice(k * tile, (k + 1) * tile)
            residue = (
                (predicted[row * panel_tiles + col] - ratings[step, k].astype(F32)) * live
            ).astype(BF16)
            picked_items[place] = panel[col]
            picked_users[place] = user_table[row]
            for u in range(user_tiles):
                by_user[u * tile : (u + 1) * tile, place] = residue * hot(row, u)
            for p in range(panel_tiles):
                by_item[place, p * tile : (p + 1) * tile] = residue * hot(col, p)
        for q in range(user_tiles // 2):
            both = slice(2 * q * tile, 2 * (q + 1) * tile)
            user_sum[both] += jnp.dot(
                by_user[both], picked_items[...], preferred_element_type=F32
            )

            @pl.when(step == n_blk - 1)
            def _(q=q):
                pair_copy(q).start()

        item_send[step] = lax.dot_general(
            by_item[...],
            picked_users[...],
            (((0,), (0,)), ((), ())),
            preferred_element_type=F32,
        )

        @pl.when(step > 0)
        def _():
            item_copy(step).start()

        return carry

    lax.fori_loop(0, n_blk, visit, 0)

    def hop(t, carry):
        @pl.when(t < chunks)
        def _():
            c = t

            @pl.when(c % per_tile == 0)
            def _():
                pair_copy(c // per_tile).wait_recv()

            mine = pair_recv.at[pl.ds(c * CHUNK, CHUNK)]
            mine[...] += user_sum[own_rows(c, core)]

            @pl.when(has_near)
            def _():
                arrived(0, c).wait_recv()

            side_send[0, c] = mine[...] + side_recv[0, c]
            far_copy(c).start()

        @pl.when(t >= LAG)
        def _():
            c = t - LAG
            mine = pair_recv.at[pl.ds(c * CHUNK, CHUNK)]
            arrived(1, c).wait_recv()

            @pl.when(has_near)
            def _():
                side_send[1, c] = mine[...] + side_recv[1, c]
                near_copy(c).start()

            user_out[own_rows(c, core)] = (
                mine[...] + side_recv[0, c] + side_recv[1, c]
            ) * (1.0 / tile)
            share_copy(c).start()

        return carry

    lax.fori_loop(0, chunks + LAG, hop, 0)

    def settle(step, carry):
        item_copy(step).wait_recv()
        item_send[0] += item_recv[step]
        return carry

    lax.fori_loop(1, n_blk, settle, 0)
    item_out[...] = item_send[0] * (1.0 / tile)

    def drain_steps(step, carry):
        gather_copy(step).wait_send()
        item_copy(step).wait_send()
        return carry

    lax.fori_loop(1, n_blk, drain_steps, 0)

    def drain_pairs(q, carry):
        pair_copy(q).wait_send()
        return carry

    lax.fori_loop(0, user_tiles // 2, drain_pairs, 0)

    def drain_chunks(c, carry):
        far_copy(c).wait_send()

        @pl.when(has_near)
        def _():
            near_copy(c).wait_send()

        share_copy(c).wait_send()
        share_arrival(c).wait_recv()
        return carry

    lax.fori_loop(0, chunks, drain_chunks, 0)


def body(user_factors, item_factors, ratings, tile_user, tile_item, tile_count):
    n_blk = lax.axis_size("blk")
    n_strata = lax.axis_size("strata")
    user_rows, rank = user_factors.shape
    panel_rows = item_factors.shape[0]
    slots, tile = ratings.shape[-3], ratings.shape[-1]
    user_tiles, panel_tiles = user_rows // tile, panel_rows // tile
    chunks = user_rows // 2 // CHUNK
    dma = pltpu.SemaphoreType.DMA
    return pl.pallas_call(
        functools.partial(kernel, n_blk, n_strata),
        out_shape=(
            jax.ShapeDtypeStruct((user_rows, rank), F32),
            jax.ShapeDtypeStruct((panel_rows, rank), F32),
        ),
        in_specs=[pl.BlockSpec(memory_space=pl.ANY)] * 3
        + [pl.BlockSpec(memory_space=pltpu.SMEM)] * 3,
        out_specs=(
            pl.BlockSpec(memory_space=pltpu.VMEM),
            pl.BlockSpec(memory_space=pltpu.VMEM),
        ),
        scratch_shapes=[
            pltpu.VMEM((user_rows, rank), BF16),
            pltpu.VMEM((user_tiles, tile, rank), BF16),
            pltpu.VMEM((n_blk, panel_rows, rank), BF16),
            pltpu.VMEM((panel_tiles, tile, rank), BF16),
            pltpu.VMEM((n_blk, slots, tile, tile), BF16),
            pltpu.VMEM((user_tiles * panel_tiles, tile, tile), F32),
            pltpu.VMEM((slots * tile, rank), BF16),
            pltpu.VMEM((slots * tile, rank), BF16),
            pltpu.VMEM((user_rows, slots * tile), BF16),
            pltpu.VMEM((slots * tile, panel_rows), BF16),
            pltpu.VMEM((user_rows, rank), F32),
            pltpu.VMEM((n_blk, panel_rows, rank), F32),
            pltpu.VMEM((n_blk, panel_rows, rank), F32),
            pltpu.VMEM((user_rows // 2, rank), F32),
            pltpu.VMEM((2, chunks, CHUNK, rank), F32),
            pltpu.VMEM((2, chunks, CHUNK, rank), F32),
            dma((2,)),
            dma((n_blk,)),
            dma((n_blk,)),
            dma((n_blk,)),
            dma((n_blk,)),
            dma((n_blk,)),
            dma((user_tiles // 2,)),
            dma((user_tiles // 2,)),
            dma((2, chunks)),
            dma((2, chunks)),
            dma((chunks,)),
            dma((chunks,)),
        ],
        compiler_params=pltpu.CompilerParams(
            collective_id=0, has_side_effects=True, vmem_limit_bytes=48 << 20
        ),
    )(user_factors, item_factors, ratings, tile_user, tile_item, tile_count)


def solution(mesh):
    in_specs = (
        P("blk", None),
        P(("blk", "strata"), None),
        P("blk", None, "strata", None, None, None),
        P("blk", None, "strata", None),
        P("blk", None, "strata", None),
        P("blk", None, "strata"),
    )
    out_specs = (P("blk", None), P(("blk", "strata"), None))
    return jax.shard_map(body, mesh=mesh, in_specs=in_specs, out_specs=out_specs, check_vma=False)
```

```python
import functools

import jax
import jax.numpy as jnp
from jax import lax
from jax.experimental import pallas as pl
from jax.experimental.pallas import tpu as pltpu
from jax.sharding import PartitionSpec as P

MESH = pl.DeviceIdType.MESH
F32 = jnp.float32
BF16 = jnp.bfloat16
CHUNK = 64
LAG = 3
STEP_LAG = 5


def flip(place, step, size):
    other, bit = 0, 1
    while bit < size:
        other = other + bit * ((place // bit + step // bit) % 2)
        bit *= 2
    return other


def kernel(
    n_blk,
    n_strata,
    users_hbm,
    items_hbm,
    ratings_hbm,
    rows_ref,
    cols_ref,
    count_ref,
    user_out,
    item_out,
    users,
    user_table,
    panels,
    panel,
    ratings,
    predicted,
    picked_items,
    picked_users,
    by_user,
    by_item,
    user_sum,
    item_send,
    item_recv,
    pair_recv,
    side_recv,
    side_send,
    load_sem,
    rating_sem,
    gather_send,
    gather_recv,
    item_send_sem,
    item_recv_sem,
    pair_send_sem,
    pair_recv_sem,
    side_send_sem,
    side_recv_sem,
    share_send_sem,
    share_recv_sem,
):
    tile = ratings.shape[-1]
    slots = ratings.shape[1]
    user_tiles = user_table.shape[0]
    panel_tiles = panel.shape[0]
    chunks = pair_recv.shape[0] // CHUNK
    per_tile = tile // CHUNK
    blk = lax.axis_index("blk")
    strata = lax.axis_index("strata")
    core = strata % 2
    sibling = strata + 1 - 2 * core
    chip = strata // 2
    chips = n_strata // 2
    half = chips // 2
    upper = chip // half
    sign = 1 - 2 * upper
    far = (chip + sign) * 2 + core
    near = (chip - sign) * 2 + core
    depth = chip + upper * (chips - 1 - 2 * chip)
    has_near = depth > 0
    lag = LAG + STEP_LAG * (half - 1 - depth)
    crossing = depth // (half - 1) if half > 1 else depth + 1

    load = pltpu.make_async_copy(users_hbm, users, load_sem.at[0])
    load.start()
    load_panel = pltpu.make_async_copy(items_hbm, panels.at[0], load_sem.at[1])
    load_panel.start()

    def rating_copy(step):
        source = flip(blk, step, n_blk)
        return pltpu.make_async_copy(
            ratings_hbm.at[0, source, 0], ratings.at[step], rating_sem.at[step]
        )

    def start_rating(step, carry):
        rating_copy(step).start()
        return carry

    lax.fori_loop(0, n_blk, start_rating, 0)

    barrier = pltpu.get_barrier_semaphore()

    def greet(step, carry):
        pl.semaphore_signal(
            barrier, 1, device_id=(flip(blk, step, n_blk), strata), device_id_type=MESH
        )
        return carry

    lax.fori_loop(1, n_blk, greet, 0)
    pl.semaphore_signal(barrier, 1, device_id=(blk, sibling), device_id_type=MESH)
    pl.semaphore_signal(barrier, 1, device_id=(blk, far), device_id_type=MESH)

    @pl.when(has_near)
    def _():
        pl.semaphore_signal(barrier, 1, device_id=(blk, near), device_id_type=MESH)
        pl.semaphore_wait(barrier, n_blk + 2)

    @pl.when(depth == 0)
    def _():
        pl.semaphore_wait(barrier, n_blk + 1)

    def gather_copy(step):
        return pltpu.make_async_remote_copy(
            src_ref=items_hbm,
            dst_ref=panels.at[step],
            send_sem=gather_send.at[step],
            recv_sem=gather_recv.at[step],
            device_id=(flip(blk, step, n_blk), strata),
            device_id_type=MESH,
        )

    def item_copy(step):
        return pltpu.make_async_remote_copy(
            src_ref=item_send.at[step],
            dst_ref=item_recv.at[step],
            send_sem=item_send_sem.at[step],
            recv_sem=item_recv_sem.at[step],
            device_id=(flip(blk, step, n_blk), strata),
            device_id_type=MESH,
        )

    def pair_copy(q):
        return pltpu.make_async_remote_copy(
            src_ref=user_sum.at[pl.ds((2 * q + 1 - core) * tile, tile)],
            dst_ref=pair_recv.at[pl.ds(q * tile, tile)],
            send_sem=pair_send_sem.at[q],
            recv_sem=pair_recv_sem.at[q],
            device_id=(blk, sibling),
            device_id_type=MESH,
        )

    def far_copy(c):
        return pltpu.make_async_remote_copy(
            src_ref=side_send.at[0, c],
            dst_ref=side_recv.at[crossing, c],
            send_sem=side_send_sem.at[0, c],
            recv_sem=side_recv_sem.at[crossing, c],
            device_id=(blk, far),
            device_id_type=MESH,
        )

    def near_copy(c):
        return pltpu.make_async_remote_copy(
            src_ref=side_send.at[1, c],
            dst_ref=side_recv.at[1, c],
            send_sem=side_send_sem.at[1, c],
            recv_sem=side_recv_sem.at[1, c],
            device_id=(blk, near),
            device_id_type=MESH,
        )

    def arrived(side, c):
        return pltpu.make_async_remote_copy(
            src_ref=side_send.at[0, c],
            dst_ref=side_recv.at[side, c],
            send_sem=side_send_sem.at[0, c],
            recv_sem=side_recv_sem.at[side, c],
            device_id=(blk, far),
            device_id_type=MESH,
        )

    def own_rows(c, owner):
        return pl.ds((2 * (c // per_tile) + owner) * tile + (c % per_tile) * CHUNK, CHUNK)

    def share_copy(c):
        return pltpu.make_async_remote_copy(
            src_ref=user_out.at[own_rows(c, core)],
            dst_ref=user_out.at[own_rows(c, core)],
            send_sem=share_send_sem.at[c],
            recv_sem=share_recv_sem.at[c],
            device_id=(blk, sibling),
            device_id_type=MESH,
        )

    def share_arrival(c):
        return pltpu.make_async_remote_copy(
            src_ref=user_out.at[own_rows(c, core)],
            dst_ref=user_out.at[own_rows(c, 1 - core)],
            send_sem=share_send_sem.at[c],
            recv_sem=share_recv_sem.at[c],
            device_id=(blk, sibling),
            device_id_type=MESH,
        )

    def start_gather(step, carry):
        gather_copy(step).start()
        return carry

    lax.fori_loop(1, n_blk, start_gather, 0)
    user_sum[...] = jnp.zeros_like(user_sum)

    @pl.when(depth == 0)
    def _():
        side_recv[0] = jnp.zeros(side_recv.shape[1:], F32)

    load.wait()
    load_panel.wait()

    user_table[...] = users[...].reshape(user_table.shape)

    def hot(index, place):
        same = (index == place).astype(F32)
        return jnp.full((tile, tile), same, F32).astype(BF16)

    def visit(step, carry):
        source = flip(blk, step, n_blk)

        @pl.when(step > 0)
        def _():
            gather_copy(step).wait_recv()

        rating_copy(step).wait()
        panel[...] = panels[step].reshape(panel.shape)
        for u in range(user_tiles):
            product = lax.dot_general(
                users[u * tile : (u + 1) * tile],
                panels[step],
                (((1,), (1,)), ((), ())),
                preferred_element_type=F32,
            )
            for p in range(panel_tiles):
                predicted[u * panel_tiles + p] = product[:, p * tile : (p + 1) * tile]
        for k in range(slots):
            row = rows_ref[0, source, 0, k]
            col = cols_ref[0, source, 0, k]
            live = (k < count_ref[0, source, 0]).astype(F32)
            place = slice(k * tile, (k + 1) * tile)
            residue = (
                (predicted[row * panel_tiles + col] - ratings[step, k].astype(F32)) * live
            ).astype(BF16)
            picked_items[place] = panel[col]
            picked_users[place] = user_table[row]
            for u in range(user_tiles):
                by_user[u * tile : (u + 1) * tile, place] = residue * hot(row, u)
            for p in range(panel_tiles):
                by_item[place, p * tile : (p + 1) * tile] = residue * hot(col, p)
        for q in range(user_tiles // 2):
            both = slice(2 * q * tile, 2 * (q + 1) * tile)
            user_sum[both] += jnp.dot(
                by_user[both], picked_items[...], preferred_element_type=F32
            )

            @pl.when(step == n_blk - 1)
            def _(q=q):
                pair_copy(q).start()

        item_send[step] = lax.dot_general(
            by_item[...],
            picked_users[...],
            (((0,), (0,)), ((), ())),
            preferred_element_type=F32,
        )

        @pl.when(step > 0)
        def _():
            item_copy(step).start()

        return carry

    lax.fori_loop(0, n_blk, visit, 0)

    def hop(t, carry):
        @pl.when(t < chunks)
        def _():
            c = t

            @pl.when(c % per_tile == 0)
            def _():
                pair_copy(c // per_tile).wait_recv()

            mine = pair_recv.at[pl.ds(c * CHUNK, CHUNK)]
            mine[...] += user_sum[own_rows(c, core)]

            @pl.when(has_near)
            def _():
                arrived(0, c).wait_recv()

            side_send[0, c] = mine[...] + side_recv[0, c]
            far_copy(c).start()

        @pl.when(t >= lag)
        def _():
            c = t - lag
            mine = pair_recv.at[pl.ds(c * CHUNK, CHUNK)]
            arrived(1, c).wait_recv()

            @pl.when(has_near)
            def _():
                side_send[1, c] = mine[...] + side_recv[1, c]
                near_copy(c).start()

            user_out[own_rows(c, core)] = (
                mine[...] + side_recv[0, c] + side_recv[1, c]
            ) * (1.0 / tile)
            share_copy(c).start()

        return carry

    lax.fori_loop(0, chunks + lag, hop, 0)

    def settle(step, carry):
        item_copy(step).wait_recv()
        item_send[0] += item_recv[step]
        return carry

    lax.fori_loop(1, n_blk, settle, 0)
    item_out[...] = item_send[0] * (1.0 / tile)

    def drain_steps(step, carry):
        gather_copy(step).wait_send()
        item_copy(step).wait_send()
        return carry

    lax.fori_loop(1, n_blk, drain_steps, 0)

    def drain_pairs(q, carry):
        pair_copy(q).wait_send()
        return carry

    lax.fori_loop(0, user_tiles // 2, drain_pairs, 0)

    def drain_chunks(c, carry):
        far_copy(c).wait_send()

        @pl.when(has_near)
        def _():
            near_copy(c).wait_send()

        share_copy(c).wait_send()
        share_arrival(c).wait_recv()
        return carry

    lax.fori_loop(0, chunks, drain_chunks, 0)


def body(user_factors, item_factors, ratings, tile_user, tile_item, tile_count):
    n_blk = lax.axis_size("blk")
    n_strata = lax.axis_size("strata")
    user_rows, rank = user_factors.shape
    panel_rows = item_factors.shape[0]
    slots, tile = ratings.shape[-3], ratings.shape[-1]
    user_tiles, panel_tiles = user_rows // tile, panel_rows // tile
    chunks = user_rows // 2 // CHUNK
    dma = pltpu.SemaphoreType.DMA
    return pl.pallas_call(
        functools.partial(kernel, n_blk, n_strata),
        out_shape=(
            jax.ShapeDtypeStruct((user_rows, rank), F32),
            jax.ShapeDtypeStruct((panel_rows, rank), F32),
        ),
        in_specs=[pl.BlockSpec(memory_space=pltpu.HBM)] * 3
        + [pl.BlockSpec(memory_space=pltpu.SMEM)] * 3,
        out_specs=(
            pl.BlockSpec(memory_space=pltpu.VMEM),
            pl.BlockSpec(memory_space=pltpu.VMEM),
        ),
        scratch_shapes=[
            pltpu.VMEM((user_rows, rank), BF16),
            pltpu.VMEM((user_tiles, tile, rank), BF16),
            pltpu.VMEM((n_blk, panel_rows, rank), BF16),
            pltpu.VMEM((panel_tiles, tile, rank), BF16),
            pltpu.VMEM((n_blk, slots, tile, tile), BF16),
            pltpu.VMEM((user_tiles * panel_tiles, tile, tile), F32),
            pltpu.VMEM((slots * tile, rank), BF16),
            pltpu.VMEM((slots * tile, rank), BF16),
            pltpu.VMEM((user_rows, slots * tile), BF16),
            pltpu.VMEM((slots * tile, panel_rows), BF16),
            pltpu.VMEM((user_rows, rank), F32),
            pltpu.VMEM((n_blk, panel_rows, rank), F32),
            pltpu.VMEM((n_blk, panel_rows, rank), F32),
            pltpu.VMEM((user_rows // 2, rank), F32),
            pltpu.VMEM((2, chunks, CHUNK, rank), F32),
            pltpu.VMEM((2, chunks, CHUNK, rank), F32),
            dma((2,)),
            dma((n_blk,)),
            dma((n_blk,)),
            dma((n_blk,)),
            dma((n_blk,)),
            dma((n_blk,)),
            dma((user_tiles // 2,)),
            dma((user_tiles // 2,)),
            dma((2, chunks)),
            dma((2, chunks)),
            dma((chunks,)),
            dma((chunks,)),
        ],
        compiler_params=pltpu.CompilerParams(
            collective_id=0, has_side_effects=True, vmem_limit_bytes=48 << 20
        ),
    )(user_factors, item_factors, ratings, tile_user, tile_item, tile_count)


def solution(mesh):
    in_specs = (
        P("blk", None),
        P(("blk", "strata"), None),
        P("blk", None, "strata", None, None, None),
        P("blk", None, "strata", None),
        P("blk", None, "strata", None),
        P("blk", None, "strata"),
    )
    out_specs = (P("blk", None), P(("blk", "strata"), None))
    return jax.shard_map(body, mesh=mesh, in_specs=in_specs, out_specs=out_specs, check_vma=False)
```

```python
import functools

import jax
import jax.numpy as jnp
from jax import lax
from jax.experimental import pallas as pl
from jax.experimental.pallas import tpu as pltpu
from jax.sharding import PartitionSpec as P

MESH = pl.DeviceIdType.MESH
F32 = jnp.float32
BF16 = jnp.bfloat16
CHUNK = 64
LAG = 2
STEP_LAG = 6


def flip(place, step, size):
    other, bit = 0, 1
    while bit < size:
        other = other + bit * ((place // bit + step // bit) % 2)
        bit *= 2
    return other


def kernel(
    n_blk,
    n_strata,
    users_hbm,
    items_hbm,
    ratings_hbm,
    rows_ref,
    cols_ref,
    count_ref,
    user_out,
    item_out,
    users,
    user_table,
    panels,
    ratings,
    predicted,
    picked_users,
    by_item,
    user_sum,
    parts,
    item_send,
    item_recv,
    pair_recv,
    side_recv,
    side_send,
    load_sem,
    rating_sem,
    gather_send,
    gather_recv,
    item_send_sem,
    item_recv_sem,
    pair_send_sem,
    pair_recv_sem,
    side_send_sem,
    side_recv_sem,
    share_send_sem,
    share_recv_sem,
):
    tile = ratings.shape[-1]
    slots = ratings.shape[1]
    user_tiles = user_table.shape[0]
    panel_tiles = panels.shape[1] // tile
    chunks = pair_recv.shape[0] // CHUNK
    per_tile = tile // CHUNK
    blk = lax.axis_index("blk")
    strata = lax.axis_index("strata")
    core = strata % 2
    sibling = strata + 1 - 2 * core
    chip = strata // 2
    chips = n_strata // 2
    half = chips // 2
    upper = chip // half
    sign = 1 - 2 * upper
    far = (chip + sign) * 2 + core
    near = (chip - sign) * 2 + core
    depth = chip + upper * (chips - 1 - 2 * chip)
    has_near = depth > 0
    lag = LAG + STEP_LAG * (half - 1 - depth)
    crossing = depth // (half - 1) if half > 1 else depth + 1

    load = pltpu.make_async_copy(users_hbm, users, load_sem.at[0])
    load.start()
    load_panel = pltpu.make_async_copy(items_hbm, panels.at[0], load_sem.at[1])
    load_panel.start()

    def rating_copy(step):
        source = flip(blk, step, n_blk)
        return pltpu.make_async_copy(
            ratings_hbm.at[0, source, 0], ratings.at[step], rating_sem.at[step]
        )

    def start_rating(step, carry):
        rating_copy(step).start()
        return carry

    lax.fori_loop(0, n_blk, start_rating, 0)

    barrier = pltpu.get_barrier_semaphore()

    def greet(step, carry):
        pl.semaphore_signal(
            barrier, 1, device_id=(flip(blk, step, n_blk), strata), device_id_type=MESH
        )
        return carry

    lax.fori_loop(1, n_blk, greet, 0)
    pl.semaphore_signal(barrier, 1, device_id=(blk, sibling), device_id_type=MESH)
    pl.semaphore_signal(barrier, 1, device_id=(blk, far), device_id_type=MESH)

    @pl.when(has_near)
    def _():
        pl.semaphore_signal(barrier, 1, device_id=(blk, near), device_id_type=MESH)
        pl.semaphore_wait(barrier, n_blk + 2)

    @pl.when(depth == 0)
    def _():
        pl.semaphore_wait(barrier, n_blk + 1)

    def gather_copy(step):
        return pltpu.make_async_remote_copy(
            src_ref=items_hbm,
            dst_ref=panels.at[step],
            send_sem=gather_send.at[step],
            recv_sem=gather_recv.at[step],
            device_id=(flip(blk, step, n_blk), strata),
            device_id_type=MESH,
        )

    def item_copy(step):
        return pltpu.make_async_remote_copy(
            src_ref=item_send.at[step],
            dst_ref=item_recv.at[step],
            send_sem=item_send_sem.at[step],
            recv_sem=item_recv_sem.at[step],
            device_id=(flip(blk, step, n_blk), strata),
            device_id_type=MESH,
        )

    def pair_copy(q):
        return pltpu.make_async_remote_copy(
            src_ref=user_sum.at[pl.ds((2 * q + 1 - core) * tile, tile)],
            dst_ref=pair_recv.at[pl.ds(q * tile, tile)],
            send_sem=pair_send_sem.at[q],
            recv_sem=pair_recv_sem.at[q],
            device_id=(blk, sibling),
            device_id_type=MESH,
        )

    def far_copy(c):
        return pltpu.make_async_remote_copy(
            src_ref=side_send.at[0, c],
            dst_ref=side_recv.at[crossing, c],
            send_sem=side_send_sem.at[0, c],
            recv_sem=side_recv_sem.at[crossing, c],
            device_id=(blk, far),
            device_id_type=MESH,
        )

    def near_copy(c):
        return pltpu.make_async_remote_copy(
            src_ref=side_send.at[1, c],
            dst_ref=side_recv.at[1, c],
            send_sem=side_send_sem.at[1, c],
            recv_sem=side_recv_sem.at[1, c],
            device_id=(blk, near),
            device_id_type=MESH,
        )

    def arrived(side, c):
        return pltpu.make_async_remote_copy(
            src_ref=side_send.at[0, c],
            dst_ref=side_recv.at[side, c],
            send_sem=side_send_sem.at[0, c],
            recv_sem=side_recv_sem.at[side, c],
            device_id=(blk, far),
            device_id_type=MESH,
        )

    def own_rows(c, owner):
        return pl.ds((2 * (c // per_tile) + owner) * tile + (c % per_tile) * CHUNK, CHUNK)

    def share_copy(c):
        return pltpu.make_async_remote_copy(
            src_ref=user_out.at[own_rows(c, core)],
            dst_ref=user_out.at[own_rows(c, core)],
            send_sem=share_send_sem.at[c],
            recv_sem=share_recv_sem.at[c],
            device_id=(blk, sibling),
            device_id_type=MESH,
        )

    def share_arrival(c):
        return pltpu.make_async_remote_copy(
            src_ref=user_out.at[own_rows(c, core)],
            dst_ref=user_out.at[own_rows(c, 1 - core)],
            send_sem=share_send_sem.at[c],
            recv_sem=share_recv_sem.at[c],
            device_id=(blk, sibling),
            device_id_type=MESH,
        )

    def start_gather(step, carry):
        gather_copy(step).start()
        return carry

    lax.fori_loop(1, n_blk, start_gather, 0)

    @pl.when(depth == 0)
    def _():
        side_recv[0] = jnp.zeros(side_recv.shape[1:], F32)

    load.wait()
    load_panel.wait()

    user_table[...] = users[...].reshape(user_table.shape)

    def hot(index, place):
        same = (index == place).astype(F32)
        return jnp.full((tile, tile), same, F32).astype(BF16)

    def visit(step, carry):
        source = flip(blk, step, n_blk)

        @pl.when(step > 0)
        def _():
            gather_copy(step).wait_recv()

        rating_copy(step).wait()
        for u in range(user_tiles):
            product = lax.dot_general(
                users[u * tile : (u + 1) * tile],
                panels[step],
                (((1,), (1,)), ((), ())),
                preferred_element_type=F32,
            )
            for p in range(panel_tiles):
                predicted[u * panel_tiles + p] = product[:, p * tile : (p + 1) * tile]
        for k in range(slots):
            row = rows_ref[0, source, 0, k]
            col = cols_ref[0, source, 0, k]
            live = (k < count_ref[0, source, 0]).astype(F32)
            place = slice(k * tile, (k + 1) * tile)
            residue = (
                (predicted[row * panel_tiles + col] - ratings[step, k].astype(F32)) * live
            ).astype(BF16)
            picked_users[place] = user_table[row]
            for p in range(panel_tiles):
                by_item[place, p * tile : (p + 1) * tile] = residue * hot(col, p)
        parts[step] = jnp.dot(by_item[...], panels[step], preferred_element_type=F32)
        item_send[step] = lax.dot_general(
            by_item[...],
            picked_users[...],
            (((0,), (0,)), ((), ())),
            preferred_element_type=F32,
        )

        @pl.when(step > 0)
        def _():
            item_copy(step).start()

        return carry

    lax.fori_loop(0, n_blk, visit, 0)

    def gather_terms(q):
        block = tile // 2
        for start in (0, block):
            sums = [jnp.zeros((block, user_sum.shape[-1]), F32)] * 2
            for step in range(n_blk):
                source = flip(blk, step, n_blk)
                for k in range(slots):
                    row = rows_ref[0, source, 0, k]
                    term = parts[step, k * tile + start : k * tile + start + block]
                    for one in range(2):
                        same = (row == 2 * q + one).astype(F32)
                        sums[one] = sums[one] + term * same
            for one in range(2):
                user_sum[pl.ds((2 * q + one) * tile + start, block)] = sums[one]
        pair_copy(q).start()

    gather_terms(0)

    def hop(t, carry):
        @pl.when((t < chunks - per_tile) & (t % per_tile == 0))
        def _():
            gather_terms(t // per_tile + 1)

        @pl.when(t < chunks)
        def _():
            c = t

            @pl.when(c % per_tile == 0)
            def _():
                pair_copy(c // per_tile).wait_recv()

            mine = pair_recv.at[pl.ds(c * CHUNK, CHUNK)]
            mine[...] += user_sum[own_rows(c, core)]

            @pl.when(has_near)
            def _():
                arrived(0, c).wait_recv()

            side_send[0, c] = mine[...] + side_recv[0, c]
            far_copy(c).start()

        @pl.when(t >= lag)
        def _():
            c = t - lag
            mine = pair_recv.at[pl.ds(c * CHUNK, CHUNK)]
            arrived(1, c).wait_recv()

            @pl.when(has_near)
            def _():
                side_send[1, c] = mine[...] + side_recv[1, c]
                near_copy(c).start()

            user_out[own_rows(c, core)] = (
                mine[...] + side_recv[0, c] + side_recv[1, c]
            ) * (1.0 / tile)
            share_copy(c).start()

        return carry

    lax.fori_loop(0, chunks + lag, hop, 0)

    def settle(step, carry):
        item_copy(step).wait_recv()
        item_send[0] += item_recv[step]
        return carry

    lax.fori_loop(1, n_blk, settle, 0)
    item_out[...] = item_send[0] * (1.0 / tile)

    def drain_steps(step, carry):
        gather_copy(step).wait_send()
        item_copy(step).wait_send()
        return carry

    lax.fori_loop(1, n_blk, drain_steps, 0)

    def drain_pairs(q, carry):
        pair_copy(q).wait_send()
        return carry

    lax.fori_loop(0, user_tiles // 2, drain_pairs, 0)

    def drain_chunks(c, carry):
        far_copy(c).wait_send()

        @pl.when(has_near)
        def _():
            near_copy(c).wait_send()

        share_copy(c).wait_send()
        share_arrival(c).wait_recv()
        return carry

    lax.fori_loop(0, chunks, drain_chunks, 0)


def body(user_factors, item_factors, ratings, tile_user, tile_item, tile_count):
    n_blk = lax.axis_size("blk")
    n_strata = lax.axis_size("strata")
    user_rows, rank = user_factors.shape
    panel_rows = item_factors.shape[0]
    slots, tile = ratings.shape[-3], ratings.shape[-1]
    user_tiles, panel_tiles = user_rows // tile, panel_rows // tile
    chunks = user_rows // 2 // CHUNK
    dma = pltpu.SemaphoreType.DMA
    return pl.pallas_call(
        functools.partial(kernel, n_blk, n_strata),
        out_shape=(
            jax.ShapeDtypeStruct((user_rows, rank), F32),
            jax.ShapeDtypeStruct((panel_rows, rank), F32),
        ),
        in_specs=[pl.BlockSpec(memory_space=pltpu.HBM)] * 3
        + [pl.BlockSpec(memory_space=pltpu.SMEM)] * 3,
        out_specs=(
            pl.BlockSpec(memory_space=pltpu.VMEM),
            pl.BlockSpec(memory_space=pltpu.VMEM),
        ),
        scratch_shapes=[
            pltpu.VMEM((user_rows, rank), BF16),
            pltpu.VMEM((user_tiles, tile, rank), BF16),
            pltpu.VMEM((n_blk, panel_rows, rank), BF16),
            pltpu.VMEM((n_blk, slots, tile, tile), BF16),
            pltpu.VMEM((user_tiles * panel_tiles, tile, tile), F32),
            pltpu.VMEM((slots * tile, rank), BF16),
            pltpu.VMEM((slots * tile, panel_rows), BF16),
            pltpu.VMEM((user_rows, rank), F32),
            pltpu.VMEM((n_blk, slots * tile, rank), F32),
            pltpu.VMEM((n_blk, panel_rows, rank), F32),
            pltpu.VMEM((n_blk, panel_rows, rank), F32),
            pltpu.VMEM((user_rows // 2, rank), F32),
            pltpu.VMEM((2, chunks, CHUNK, rank), F32),
            pltpu.VMEM((2, chunks, CHUNK, rank), F32),
            dma((2,)),
            dma((n_blk,)),
            dma((n_blk,)),
            dma((n_blk,)),
            dma((n_blk,)),
            dma((n_blk,)),
            dma((user_tiles // 2,)),
            dma((user_tiles // 2,)),
            dma((2, chunks)),
            dma((2, chunks)),
            dma((chunks,)),
            dma((chunks,)),
        ],
        compiler_params=pltpu.CompilerParams(
            collective_id=0, has_side_effects=True, vmem_limit_bytes=60 << 20
        ),
    )(user_factors, item_factors, ratings, tile_user, tile_item, tile_count)


def solution(mesh):
    in_specs = (
        P("blk", None),
        P(("blk", "strata"), None),
        P("blk", None, "strata", None, None, None),
        P("blk", None, "strata", None),
        P("blk", None, "strata", None),
        P("blk", None, "strata"),
    )
    out_specs = (P("blk", None), P(("blk", "strata"), None))
    return jax.shard_map(body, mesh=mesh, in_specs=in_specs, out_specs=out_specs, check_vma=False)
```

```python
import functools

import jax
import jax.numpy as jnp
from jax import lax
from jax.experimental import pallas as pl
from jax.experimental.pallas import tpu as pltpu
from jax.sharding import PartitionSpec as P

MESH = pl.DeviceIdType.MESH
F32 = jnp.float32
BF16 = jnp.bfloat16
CHUNK = 64
LAG = 2
STEP_LAG = 6


def flip(place, step, size):
    other, bit = 0, 1
    while bit < size:
        other = other + bit * ((place // bit + step // bit) % 2)
        bit *= 2
    return other


def kernel(
    n_blk,
    n_strata,
    users_hbm,
    items_hbm,
    ratings_hbm,
    rows_ref,
    cols_ref,
    count_ref,
    user_out,
    item_out,
    users,
    user_table,
    panels,
    ratings,
    predicted,
    picked_users,
    by_item,
    user_sum,
    parts,
    item_send,
    item_recv,
    pair_recv,
    side_recv,
    side_send,
    load_sem,
    rating_sem,
    gather_send,
    gather_recv,
    item_send_sem,
    item_recv_sem,
    pair_send_sem,
    pair_recv_sem,
    side_send_sem,
    side_recv_sem,
    share_send_sem,
    share_recv_sem,
):
    tile = ratings.shape[-1]
    slots = ratings.shape[1]
    user_tiles = user_table.shape[0]
    panel_tiles = panels.shape[1] // tile
    chunks = pair_recv.shape[0] // CHUNK
    per_tile = tile // CHUNK
    blk = lax.axis_index("blk")
    strata = lax.axis_index("strata")
    core = strata % 2
    sibling = strata + 1 - 2 * core
    chip = strata // 2
    chips = n_strata // 2
    half = chips // 2
    upper = chip // half
    sign = 1 - 2 * upper
    far = (chip + sign) * 2 + core
    near = (chip - sign) * 2 + core
    depth = chip + upper * (chips - 1 - 2 * chip)
    has_near = depth > 0
    lag = LAG + STEP_LAG * (half - 1 - depth)
    crossing = depth // (half - 1) if half > 1 else depth + 1

    load = pltpu.make_async_copy(users_hbm, users, load_sem.at[0])
    load.start()
    load_panel = pltpu.make_async_copy(items_hbm, panels.at[0], load_sem.at[1])
    load_panel.start()

    def rating_copy(step):
        source = flip(blk, step, n_blk)
        return pltpu.make_async_copy(
            ratings_hbm.at[0, source, 0], ratings.at[step], rating_sem.at[step]
        )

    def start_rating(step, carry):
        rating_copy(step).start()
        return carry

    lax.fori_loop(0, n_blk, start_rating, 0)

    barrier = pltpu.get_barrier_semaphore()

    def greet(step, carry):
        pl.semaphore_signal(
            barrier, 1, device_id=(flip(blk, step, n_blk), strata), device_id_type=MESH
        )
        return carry

    lax.fori_loop(1, n_blk, greet, 0)
    pl.semaphore_signal(barrier, 1, device_id=(blk, sibling), device_id_type=MESH)
    pl.semaphore_signal(barrier, 1, device_id=(blk, far), device_id_type=MESH)

    @pl.when(has_near)
    def _():
        pl.semaphore_signal(barrier, 1, device_id=(blk, near), device_id_type=MESH)
        pl.semaphore_wait(barrier, n_blk + 2)

    @pl.when(depth == 0)
    def _():
        pl.semaphore_wait(barrier, n_blk + 1)

    def gather_copy(step):
        return pltpu.make_async_remote_copy(
            src_ref=items_hbm,
            dst_ref=panels.at[step],
            send_sem=gather_send.at[step],
            recv_sem=gather_recv.at[step],
            device_id=(flip(blk, step, n_blk), strata),
            device_id_type=MESH,
        )

    def item_copy(step):
        return pltpu.make_async_remote_copy(
            src_ref=item_send.at[step],
            dst_ref=item_recv.at[step],
            send_sem=item_send_sem.at[step],
            recv_sem=item_recv_sem.at[step],
            device_id=(flip(blk, step, n_blk), strata),
            device_id_type=MESH,
        )

    def pair_copy(q):
        return pltpu.make_async_remote_copy(
            src_ref=user_sum.at[pl.ds((2 * q + 1 - core) * tile, tile)],
            dst_ref=pair_recv.at[pl.ds(q * tile, tile)],
            send_sem=pair_send_sem.at[q],
            recv_sem=pair_recv_sem.at[q],
            device_id=(blk, sibling),
            device_id_type=MESH,
        )

    def far_copy(c):
        return pltpu.make_async_remote_copy(
            src_ref=side_send.at[0, c],
            dst_ref=side_recv.at[crossing, c],
            send_sem=side_send_sem.at[0, c],
            recv_sem=side_recv_sem.at[crossing, c],
            device_id=(blk, far),
            device_id_type=MESH,
        )

    def near_copy(c):
        return pltpu.make_async_remote_copy(
            src_ref=side_send.at[1, c],
            dst_ref=side_recv.at[1, c],
            send_sem=side_send_sem.at[1, c],
            recv_sem=side_recv_sem.at[1, c],
            device_id=(blk, near),
            device_id_type=MESH,
        )

    def arrived(side, c):
        return pltpu.make_async_remote_copy(
            src_ref=side_send.at[0, c],
            dst_ref=side_recv.at[side, c],
            send_sem=side_send_sem.at[0, c],
            recv_sem=side_recv_sem.at[side, c],
            device_id=(blk, far),
            device_id_type=MESH,
        )

    def own_rows(c, owner):
        return pl.ds((2 * (c // per_tile) + owner) * tile + (c % per_tile) * CHUNK, CHUNK)

    def share_copy(c):
        return pltpu.make_async_remote_copy(
            src_ref=user_out.at[own_rows(c, core)],
            dst_ref=user_out.at[own_rows(c, core)],
            send_sem=share_send_sem.at[c],
            recv_sem=share_recv_sem.at[c],
            device_id=(blk, sibling),
            device_id_type=MESH,
        )

    def share_arrival(c):
        return pltpu.make_async_remote_copy(
            src_ref=user_out.at[own_rows(c, core)],
            dst_ref=user_out.at[own_rows(c, 1 - core)],
            send_sem=share_send_sem.at[c],
            recv_sem=share_recv_sem.at[c],
            device_id=(blk, sibling),
            device_id_type=MESH,
        )

    def start_gather(step, carry):
        gather_copy(step).start()
        return carry

    lax.fori_loop(1, n_blk, start_gather, 0)

    @pl.when(depth == 0)
    def _():
        side_recv[0] = jnp.zeros(side_recv.shape[1:], F32)

    load.wait()
    load_panel.wait()

    user_table[...] = users[...].reshape(user_table.shape)

    def hot(index, place):
        same = (index == place).astype(F32)
        return jnp.full((tile, tile), same, F32).astype(BF16)

    def visit(step, carry):
        source = flip(blk, step, n_blk)

        @pl.when(step > 0)
        def _():
            gather_copy(step).wait_recv()

        rating_copy(step).wait()
        for u in range(user_tiles):
            product = lax.dot_general(
                users[u * tile : (u + 1) * tile],
                panels[step],
                (((1,), (1,)), ((), ())),
                preferred_element_type=F32,
            )
            for p in range(panel_tiles):
                predicted[u * panel_tiles + p] = product[:, p * tile : (p + 1) * tile]
        for k in range(slots):
            row = rows_ref[0, source, 0, k]
            col = cols_ref[0, source, 0, k]
            live = (k < count_ref[0, 0, source]).astype(F32)
            place = slice(k * tile, (k + 1) * tile)
            residue = (
                (predicted[row * panel_tiles + col] - ratings[step, k].astype(F32)) * live
            ).astype(BF16)
            picked_users[place] = user_table[row]
            for p in range(panel_tiles):
                by_item[place, p * tile : (p + 1) * tile] = residue * hot(col, p)
        parts[step] = jnp.dot(by_item[...], panels[step], preferred_element_type=F32)
        item_send[step] = lax.dot_general(
            by_item[...],
            picked_users[...],
            (((0,), (0,)), ((), ())),
            preferred_element_type=F32,
        )

        @pl.when(step > 0)
        def _():
            item_copy(step).start()

        return carry

    lax.fori_loop(0, n_blk, visit, 0)

    def gather_terms(q):
        block = tile // 2
        for start in (0, block):
            sums = [jnp.zeros((block, user_sum.shape[-1]), F32)] * 2
            for step in range(n_blk):
                source = flip(blk, step, n_blk)
                for k in range(slots):
                    row = rows_ref[0, source, 0, k]
                    term = parts[step, k * tile + start : k * tile + start + block]
                    for one in range(2):
                        same = (row == 2 * q + one).astype(F32)
                        sums[one] = sums[one] + term * same
            for one in range(2):
                user_sum[pl.ds((2 * q + one) * tile + start, block)] = sums[one]
        pair_copy(q).start()

    gather_terms(0)

    def hop(t, carry):
        @pl.when((t < chunks - per_tile) & (t % per_tile == 0))
        def _():
            gather_terms(t // per_tile + 1)

        @pl.when(t < chunks)
        def _():
            c = t

            @pl.when(c % per_tile == 0)
            def _():
                pair_copy(c // per_tile).wait_recv()

            mine = pair_recv.at[pl.ds(c * CHUNK, CHUNK)]
            mine[...] += user_sum[own_rows(c, core)]

            @pl.when(has_near)
            def _():
                arrived(0, c).wait_recv()

            side_send[0, c] = mine[...] + side_recv[0, c]
            far_copy(c).start()

        @pl.when(t >= lag)
        def _():
            c = t - lag
            mine = pair_recv.at[pl.ds(c * CHUNK, CHUNK)]
            arrived(1, c).wait_recv()

            @pl.when(has_near)
            def _():
                side_send[1, c] = mine[...] + side_recv[1, c]
                near_copy(c).start()

            user_out[own_rows(c, core)] = (
                mine[...] + side_recv[0, c] + side_recv[1, c]
            ) * (1.0 / tile)
            share_copy(c).start()

        return carry

    lax.fori_loop(0, chunks + lag, hop, 0)

    def settle(step, carry):
        item_copy(step).wait_recv()
        item_send[0] += item_recv[step]
        return carry

    lax.fori_loop(1, n_blk, settle, 0)
    item_out[...] = item_send[0] * (1.0 / tile)

    def drain_steps(step, carry):
        gather_copy(step).wait_send()
        item_copy(step).wait_send()
        return carry

    lax.fori_loop(1, n_blk, drain_steps, 0)

    def drain_pairs(q, carry):
        pair_copy(q).wait_send()
        return carry

    lax.fori_loop(0, user_tiles // 2, drain_pairs, 0)

    def drain_chunks(c, carry):
        far_copy(c).wait_send()

        @pl.when(has_near)
        def _():
            near_copy(c).wait_send()

        share_copy(c).wait_send()
        share_arrival(c).wait_recv()
        return carry

    lax.fori_loop(0, chunks, drain_chunks, 0)


def body(user_factors, item_factors, ratings, tile_user, tile_item, tile_count):
    n_blk = lax.axis_size("blk")
    n_strata = lax.axis_size("strata")
    user_rows, rank = user_factors.shape
    panel_rows = item_factors.shape[0]
    slots, tile = ratings.shape[-3], ratings.shape[-1]
    user_tiles, panel_tiles = user_rows // tile, panel_rows // tile
    chunks = user_rows // 2 // CHUNK
    dma = pltpu.SemaphoreType.DMA
    return pl.pallas_call(
        functools.partial(kernel, n_blk, n_strata),
        out_shape=(
            jax.ShapeDtypeStruct((user_rows, rank), F32),
            jax.ShapeDtypeStruct((panel_rows, rank), F32),
        ),
        in_specs=[pl.BlockSpec(memory_space=pltpu.HBM)] * 3
        + [pl.BlockSpec(memory_space=pltpu.SMEM)] * 3,
        out_specs=(
            pl.BlockSpec(memory_space=pltpu.VMEM),
            pl.BlockSpec(memory_space=pltpu.VMEM),
        ),
        scratch_shapes=[
            pltpu.VMEM((user_rows, rank), BF16),
            pltpu.VMEM((user_tiles, tile, rank), BF16),
            pltpu.VMEM((n_blk, panel_rows, rank), BF16),
            pltpu.VMEM((n_blk, slots, tile, tile), BF16),
            pltpu.VMEM((user_tiles * panel_tiles, tile, tile), F32),
            pltpu.VMEM((slots * tile, rank), BF16),
            pltpu.VMEM((slots * tile, panel_rows), BF16),
            pltpu.VMEM((user_rows, rank), F32),
            pltpu.VMEM((n_blk, slots * tile, rank), F32),
            pltpu.VMEM((n_blk, panel_rows, rank), F32),
            pltpu.VMEM((n_blk, panel_rows, rank), F32),
            pltpu.VMEM((user_rows // 2, rank), F32),
            pltpu.VMEM((2, chunks, CHUNK, rank), F32),
            pltpu.VMEM((2, chunks, CHUNK, rank), F32),
            dma((2,)),
            dma((n_blk,)),
            dma((n_blk,)),
            dma((n_blk,)),
            dma((n_blk,)),
            dma((n_blk,)),
            dma((user_tiles // 2,)),
            dma((user_tiles // 2,)),
            dma((2, chunks)),
            dma((2, chunks)),
            dma((chunks,)),
            dma((chunks,)),
        ],
        compiler_params=pltpu.CompilerParams(
            collective_id=0, has_side_effects=True, vmem_limit_bytes=48 << 20
        ),
    )(
        pltpu.with_memory_space_constraint(user_factors, pltpu.HBM),
        pltpu.with_memory_space_constraint(item_factors, pltpu.HBM),
        pltpu.with_memory_space_constraint(ratings, pltpu.HBM),
        tile_user, tile_item, jnp.swapaxes(tile_count, 1, 2))


def solution(mesh):
    in_specs = (
        P("blk", None),
        P(("blk", "strata"), None),
        P("blk", None, "strata", None, None, None),
        P("blk", None, "strata", None),
        P("blk", None, "strata", None),
        P("blk", None, "strata"),
    )
    out_specs = (P("blk", None), P(("blk", "strata"), None))
    return jax.shard_map(body, mesh=mesh, in_specs=in_specs, out_specs=out_specs, check_vma=False)
```
